32 devices in a mesh: row: 1, ang: 32 (over z, y, x, core).
Axes of the slice: x: 2, y: 2, z: 4, core: 2. Of those that a mesh axis runs over, the one named last changes fastest.
Arguments:
- linv_t: bfloat16 [2, 2048, 2048], P(None, 'ang', 'row'), may hold values from -1.5 to 1.5, as said below
- rhs_top: float32 [2, 2048, 16384], P(None, 'row', 'ang'), may hold values from -6 to 6
- factor_t: bfloat16 [2, 2048, 1024], P(None, 'ang', 'row'), may hold values from -0.125 to 0.125
- rhs_rest: float32 [2, 1024, 16384], P(None, 'row', 'ang'), may hold values from -6 to 6
Outputs:
- solved: float32 [2, 2048, 16384], P(None, 'row', 'ang')
- updated: float32 [2, 1024, 16384], P(None, 'row', 'ang')
The draws below stay inside these ranges and needn't reach their ends.
Inputs may be any that keep to these rules, and one draw needn't show every extreme that they name: `linv_t`: lower triangular inverse: entry [c, j, i] is zero where j > i; the diagonal is real and between 0.5 and 1.5.
All inputs are finite; a program needn't handle non-finite values.
Results may differ from the reference program's by a relative error of at most 0.0026.
Values may be sent and summed in bfloat16 or wider, within the bound.
A program may use at most 128 MiB of HBM per device.

```python
import math
import jax
import jax.numpy as jnp
from jax import lax

PANEL = 2048
ANG_DEV = 512
TRAIL = 1024
ANGLES = 16384
N_ANG = 32


def draw_linv_t(key, part):
    first_key, second_key = jax.random.split(jax.random.fold_in(key, 17))
    spread = jax.random.normal(first_key, (2, PANEL, PANEL), jnp.float32)
    spread = spread * (0.7 / math.sqrt(PANEL))
    col_index = lax.broadcasted_iota(jnp.int32, (PANEL, PANEL), 0)
    row_index = lax.broadcasted_iota(jnp.int32, (PANEL, PANEL), 1)
    lower = (col_index < row_index).astype(jnp.float32)
    diag_vals = jax.random.uniform(second_key, (PANEL,), jnp.float32, 0.5, 1.5)
    eye_part = (col_index == row_index).astype(jnp.float32) * diag_vals[None, :]
    real_part = spread[0] * lower + eye_part
    imag_part = spread[1] * lower
    return jnp.stack([real_part, imag_part]).astype(jnp.bfloat16)


def steps_of(key, shape, cuts, least, largest):
    level, own = 1.0, jax.random.fold_in(key, 6)
    for position, shards_of in cuts:
        heights = jnp.exp(jax.random.uniform(jax.random.fold_in(own, position), (shards_of,), jnp.float32, least / len(cuts), largest / len(cuts)))
        level = level * jnp.repeat(heights, shape[position] // shards_of).reshape([-1 if axis == position else 1 for axis in range(len(shape))])
    return level


def normal_values(key, shape, scale, most, cuts=(), held_as=jnp.bfloat16):
    array = jax.random.normal(key, shape, jnp.float32) * scale
    if len(cuts) > 0:
        array = steps_of(key, shape, cuts, -0.22, 0.18) * array
    return jnp.clip(array, min=-most, max=most).astype(held_as)


def setup_inputs(seed: int = 0) -> dict:
    keys = jax.random.split(jax.random.key(seed), 5)
    return {
        "linv_t": draw_linv_t(jax.random.fold_in(keys[4], 71), 0),
        "rhs_top": normal_values(keys[1], (2, PANEL, ANGLES), 1.0, 6.0, ((2, 32),), jnp.float32),
        "factor_t": normal_values(keys[2], (2, PANEL, TRAIL), PANEL ** -0.5, 0.125, ((1, 32),)),
        "rhs_rest": normal_values(keys[3], (2, TRAIL, ANGLES), 1.0, 6.0, ((2, 32),), jnp.float32),
    }


def complex_tdot(left, right, precision):
    dims = (((0,), (0,)), ((), ()))

    def single(first, second):
        return lax.dot_general(first, second, dims, precision=precision, preferred_element_type=jnp.float32)

    real_part = single(left[0], right[0]) - single(left[1], right[1])
    imag_part = single(left[0], right[1]) + single(left[1], right[0])
    return jnp.stack([real_part, imag_part])


def reference(linv_t, rhs_top, factor_t, rhs_rest):
    inverse = linv_t.astype(jnp.float32)
    blocks = N_ANG

    def per_block(index):
        top_block = lax.dynamic_slice_in_dim(rhs_top, index * ANG_DEV, ANG_DEV, 2)
        rest_block = lax.dynamic_slice_in_dim(rhs_rest, index * ANG_DEV, ANG_DEV, 2)
        solved = complex_tdot(inverse, top_block, lax.Precision.HIGHEST)
        update = complex_tdot(factor_t, solved.astype(jnp.bfloat16), None)
        return solved, rest_block - update

    solved_blocks, rest_blocks = lax.map(per_block, jnp.arange(blocks, dtype=jnp.int32))
    solved = jnp.moveaxis(solved_blocks, 0, 2).reshape(2, rhs_top.shape[1], rhs_top.shape[2])
    updated = jnp.moveaxis(rest_blocks, 0, 2).reshape(2, rhs_rest.shape[1], rhs_rest.shape[2])
    return solved, updated
```

```python
import functools

import jax
import jax.numpy as jnp
from jax import lax
from jax.experimental import pallas as pl
from jax.experimental.pallas import tpu as pltpu
from jax.sharding import PartitionSpec as P

LAG = 1
KINDS = ((0, 0, "zyx"), (0, 1, "zxy"), (1, 0, "yzx"), (1, 1, "xzy"))
DIMS0 = (((0,), (0,)), ((), ()))


def tdot(first, second):
    return lax.dot_general(first, second, DIMS0, preferred_element_type=jnp.float32)


def split_two(value):
    high = value.astype(jnp.bfloat16)
    low = (value - high.astype(jnp.float32)).astype(jnp.bfloat16)
    return high, low


def general_body(linv_t, rhs_top, factor_t, rhs_rest):
    top_all = lax.all_gather(rhs_top, "row", axis=1, tiled=True)
    high, low = split_two(top_all)
    inverse = lax.all_gather(linv_t, "ang", axis=1, tiled=True)

    def single(first, second):
        return tdot(inverse[first], high[second]) + tdot(inverse[first], low[second])

    solved = jnp.stack([single(0, 0) - single(1, 1), single(0, 1) + single(1, 0)])
    half = lax.all_gather(solved.astype(jnp.bfloat16), "row", axis=1, tiled=True)
    factor = lax.all_gather(factor_t, "ang", axis=1, tiled=True)
    update = jnp.stack(
        [
            tdot(factor[0], half[0]) - tdot(factor[1], half[1]),
            tdot(factor[0], half[1]) + tdot(factor[1], half[0]),
        ]
    )
    return (solved, rhs_rest - update)


def fused_kernel(
    devices, lag, lin_ref, top_ref, fac_ref, rest_ref, acc, upd,
    glin, gfac, terms, recv, send, local,
):
    levels = devices // 8
    chips = devices // 2
    rows = lin_ref.shape[1]
    panel = lin_ref.shape[2]
    width = top_ref.shape[2]
    block = 4 * rows
    blocks = panel // block
    tail = fac_ref.shape[2] // block

    me = lax.axis_index("ang")
    core = lax.rem(me, 2)
    x = lax.rem(me // 2, 2)
    y = lax.rem(me // 4, 2)
    z = me // 8
    has_up, has_down = z < levels - 1, z > 0
    targets = (
        me + 2 - 4 * x,
        me + 4 - 8 * y,
        jnp.where(has_up, me + 8, me),
        jnp.where(has_down, me - 8, me),
        me + 1 - 2 * core,
    )
    mine = pl.ds(pl.multiple_of(me * rows, rows), rows)

    loads = (
        pltpu.make_async_copy(top_ref, acc, local.at[0]),
        pltpu.make_async_copy(lin_ref, glin.at[:, mine, :], local.at[1]),
        pltpu.make_async_copy(fac_ref, gfac.at[:, mine, :], local.at[2]),
        pltpu.make_async_copy(rest_ref, upd, local.at[3]),
    )

    barrier = pltpu.get_barrier_semaphore()

    def greet(target):
        pl.semaphore_signal(
            barrier, inc=1, device_id={"ang": target}, device_id_type=pl.DeviceIdType.MESH
        )

    for index in (0, 1, 4):
        greet(targets[index])
    pl.when(has_up)(lambda: greet(targets[2]))
    pl.when(has_down)(lambda: greet(targets[3]))
    pl.semaphore_wait(barrier, 3 + has_up.astype(jnp.int32) + has_down.astype(jnp.int32))

    def block_at(index):
        return pl.ds(pl.multiple_of(index * block, block), block)

    def place(kind, origin, cls):
        which, part, _ = KINDS[kind]
        at_rows = pl.ds(pl.multiple_of(origin * rows, rows), rows)
        if which == 0:
            return glin.at[part, at_rows, pl.ds(cls * block, panel - cls * block)]
        return gfac.at[part, at_rows, :]

    def source(kind, cls):
        which, part, _ = KINDS[kind]
        if which == 0:
            return lin_ref.at[part, :, pl.ds(cls * block, panel - cls * block)]
        return fac_ref.at[part]

    def by_class(kind, origin, action):
        if KINDS[kind][0] == 0:
            for cls in range(blocks):
                pl.when(origin // 4 == cls)(functools.partial(action, cls))
        else:
            action(0)

    def remote(kind, origin, cls, direction, own):
        return pltpu.make_async_remote_copy(
            src_ref=source(kind, cls) if own else place(kind, origin, cls),
            dst_ref=place(kind, origin, cls),
            send_sem=send.at[direction, kind, origin // 2],
            recv_sem=recv.at[kind, origin],
            device_id={"ang": targets[direction]},
            device_id_type=pl.DeviceIdType.MESH,
        )

    def onward(kind, zo, yo, xo):
        same = {"x": x == xo, "y": y == yo, "z": z == zo}
        order = KINDS[kind][2]
        free = {}
        for position, axis in enumerate(order):
            ok = True
            for later in order[position + 1 :]:
                ok = same[later] if ok is True else jnp.logical_and(ok, same[later])
            free[axis] = ok

        def both(first, second):
            return second if first is True else jnp.logical_and(first, second)

        return (
            both(free["x"], same["x"]),
            both(free["y"], same["y"]),
            both(free["z"], jnp.logical_and(z >= zo, has_up)),
            both(free["z"], jnp.logical_and(z <= zo, has_down)),
            True,
        )

    def forward(kind, origin, goes, cls, own, act):
        for direction in range(5):
            copy = remote(kind, origin, cls, direction, own)
            run = copy.start if act == "start" else copy.wait_send
            if goes[direction] is True:
                run()
            else:
                pl.when(goes[direction])(run)

    def send_own(kind):
        goes = onward(kind, z, y, x)
        by_class(kind, me, lambda cls: forward(kind, me, goes, cls, True, "start"))

    def arrive_other(kind, origin):
        by_class(kind, origin, lambda cls: remote(kind, origin, cls, 4, False).wait_recv())

    send_own(0)
    send_own(1)
    for copy in loads:
        copy.start()
    loads[0].wait()

    @pl.loop(0, blocks)
    def _(index):
        at_rows = block_at(index)
        for part in range(2):
            first, second = split_two(acc[part, at_rows, :])
            terms[pl.ds(pl.multiple_of((4 * index + 2 * part) * block, block), block), :] = first
            terms[pl.ds(pl.multiple_of((4 * index + 2 * part + 1) * block, block), block), :] = second
            acc[part, at_rows, :] = jnp.zeros((block, width), jnp.float32)

    for copy in loads[1:]:
        copy.wait()

    def solve_piece(group, index):
        at_rows, to = block_at(group), block_at(index)
        lreal, limag = glin[0, at_rows, to].T, glin[1, at_rows, to].T
        right = terms[pl.ds(pl.multiple_of(4 * group * block, block), 4 * block), :]
        real = jnp.concatenate([lreal, lreal, -limag, -limag], axis=1)
        imag = jnp.concatenate([limag, limag, lreal, lreal], axis=1)
        both = jnp.dot(
            jnp.concatenate([real, imag]), right, preferred_element_type=jnp.float32
        )
        acc[0, to, :] += both[:block]
        acc[1, to, :] += both[block:]

    def update_piece(group, index):
        at_rows, to = block_at(group), block_at(index)
        freal, fimag = gfac[0, at_rows, to].T, gfac[1, at_rows, to].T
        right = terms[pl.ds(pl.multiple_of(2 * group * block, block), 2 * block), :]
        real = jnp.concatenate([freal, -fimag], axis=1)
        imag = jnp.concatenate([fimag, freal], axis=1)
        both = jnp.dot(
            jnp.concatenate([real, imag]), right, preferred_element_type=jnp.float32
        )
        upd[0, to, :] -= both[:block]
        upd[1, to, :] -= both[block:]

    def update_block(index):
        to = block_at(index)
        freal, fimag = gfac[0, :, to].T, gfac[1, :, to].T
        lines = []
        for first, second in ((freal, -fimag), (fimag, freal)):
            pieces = []
            for group in range(blocks):
                cols = slice(group * block, (group + 1) * block)
                pieces += [first[:, cols], second[:, cols]]
            lines.append(jnp.concatenate(pieces, axis=1))
        both = jnp.dot(
            jnp.concatenate(lines),
            terms[pl.ds(0, 2 * panel), :],
            preferred_element_type=jnp.float32,
        )
        upd[0, to, :] -= both[:block]
        upd[1, to, :] -= both[block:]

    last_round = levels + 2 + lag
    solved_at = levels + 3

    def apart(group):
        return jnp.abs(z - group // 2) + jnp.abs(y - lax.rem(group, 2))

    def first_round(group):
        return jnp.maximum(apart(group) + 2 + lag, solved_at)

    def solve_count(group, turn):
        return jnp.where(apart(group) + 2 == turn, blocks - group, 0)

    def update_count(group, turn):
        return jnp.where(jnp.logical_and(turn == last_round, group < tail), 1, 0)

    def run_pieces(turn, first, last):
        def find(number, count):
            def scan(group, carry):
                rest, found = carry
                size = count(group, turn)
                found = jnp.where(jnp.logical_and(found < 0, rest < size), group, found)
                return jnp.where(found < 0, rest - size, rest), found

            return lax.fori_loop(0, blocks, scan, (number, jnp.int32(-1)))

        @pl.when(turn < solved_at)
        def _():
            @pl.loop(first, last)
            def _(number):
                rest, group = find(number, solve_count)
                solve_piece(group, group + rest)

        @pl.when(turn >= solved_at)
        def _():
            @pl.loop(first, last)
            def _(number):
                rest, group = find(number, update_count)
                update_block(group)

    def distance_to(chip):
        zo, yo, xo = chip // 4, lax.rem(chip // 2, 2), lax.rem(chip, 2)
        return jnp.abs(z - zo) + jnp.abs(y - yo) + jnp.abs(x - xo)

    def in_round(chip, turn):
        distance = distance_to(chip)
        first = distance == turn
        second = jnp.logical_and(distance == turn - lag, turn > lag)
        return first, second

    def one_round(turn, carry):
        @pl.when(turn == lag)
        def _():
            send_own(2)
            send_own(3)

        @pl.when(turn == solved_at)
        def _():
            @pl.loop(0, blocks)
            def _(index):
                for part in range(2):
                    to = pl.ds(pl.multiple_of((2 * index + part) * block, block), block)
                    terms[to, :] = acc[part, block_at(index), :].astype(jnp.bfloat16)

        def arrivals(chip, carry):
            other = chip * 2 + 1 - core
            group = chip // 2

            @pl.when(apart(group) + 2 == turn)
            def _():
                arrive_other(0, other)
                arrive_other(1, other)

            @pl.when(first_round(group) == turn)
            def _():
                arrive_other(2, other)
                arrive_other(3, other)

            return carry

        lax.fori_loop(0, chips, arrivals, 0)

        def add_pieces(group, total):
            return total + jnp.where(
                turn < solved_at, solve_count(group, turn), update_count(group, turn)
            )

        def add_events(chip, total):
            first, second = in_round(chip, turn)
            return total + jnp.where(jnp.logical_or(first, second), 1, 0)

        pieces = lax.fori_loop(0, blocks, add_pieces, jnp.int32(0))
        slots = lax.fori_loop(0, chips, add_events, jnp.int32(1))

        def visit(chip, slot):
            zo, yo, xo = chip // 4, lax.rem(chip // 2, 2), lax.rem(chip, 2)
            origin = chip * 2 + core
            first, second = in_round(chip, turn)
            either = jnp.logical_or(first, second)

            for kinds, now in (((0, 1), first), ((2, 3), second)):

                @pl.when(now)
                def _(kinds=kinds):
                    for kind in kinds:
                        goes = onward(kind, zo, yo, xo)

                        def arrive(cls, kind=kind, goes=goes):
                            remote(kind, origin, cls, 4, False).wait_recv()
                            forward(kind, origin, goes, cls, False, "start")

                        by_class(kind, origin, arrive)

            @pl.when(either)
            def _():
                run_pieces(turn, slot * pieces // slots, (slot + 1) * pieces // slots)

            return slot + jnp.where(either, 1, 0)

        lax.fori_loop(0, chips, visit, jnp.int32(0))
        run_pieces(turn, (slots - 1) * pieces // slots, pieces)
        return carry

    lax.fori_loop(1, levels + 3 + lag, one_round, 0)

    def finish(chip, carry):
        zo, yo, xo = chip // 4, lax.rem(chip // 2, 2), lax.rem(chip, 2)
        origin = chip * 2 + core
        for kind in range(4):
            goes = onward(kind, zo, yo, xo)
            by_class(
                kind,
                origin,
                lambda cls, kind=kind, goes=goes: forward(kind, origin, goes, cls, False, "wait"),
            )
        return carry

    lax.fori_loop(0, chips, finish, 0)


def store_kernel(acc, upd, solved_ref, updated_ref, sems):
    stores = (
        pltpu.make_async_copy(acc, solved_ref, sems.at[0]),
        pltpu.make_async_copy(upd, updated_ref, sems.at[1]),
    )
    for copy in stores:
        copy.start()
    for copy in stores:
        copy.wait()


def fused_body(devices, linv_t, rhs_top, factor_t, rhs_rest):
    parts, rows, panel = linv_t.shape
    trail, width = rhs_rest.shape[1:]
    held = pl.pallas_call(
        functools.partial(fused_kernel, devices, LAG),
        out_shape=(
            pltpu.VMEM(rhs_top.shape, jnp.float32),
            pltpu.VMEM(rhs_rest.shape, jnp.float32),
        ),
        in_specs=[pl.BlockSpec(memory_space=pl.ANY)] * 4,
        out_specs=[pl.BlockSpec(memory_space=pltpu.VMEM)] * 2,
        scratch_shapes=[
            pltpu.VMEM((parts, panel, panel), linv_t.dtype),
            pltpu.VMEM((parts, panel, trail), factor_t.dtype),
            pltpu.VMEM((4 * panel, width), jnp.bfloat16),
            pltpu.SemaphoreType.DMA((4, devices)),
            pltpu.SemaphoreType.DMA((5, 4, devices // 2)),
            pltpu.SemaphoreType.DMA((4,)),
        ],
        compiler_params=pltpu.CompilerParams(
            collective_id=0, has_side_effects=True, vmem_limit_bytes=48 << 20
        ),
    )(linv_t, rhs_top, factor_t, rhs_rest)
    return pl.pallas_call(
        store_kernel,
        out_shape=(
            jax.ShapeDtypeStruct(rhs_top.shape, jnp.float32),
            jax.ShapeDtypeStruct(rhs_rest.shape, jnp.float32),
        ),
        in_specs=[pl.BlockSpec(memory_space=pltpu.VMEM)] * 2,
        out_specs=[pl.BlockSpec(memory_space=pl.ANY)] * 2,
        scratch_shapes=[pltpu.SemaphoreType.DMA((2,))],
        compiler_params=pltpu.CompilerParams(vmem_limit_bytes=8 << 20),
    )(*(pltpu.with_memory_space_constraint(array, pltpu.VMEM) for array in held))


def solution(mesh):
    devices = mesh.shape["ang"]
    if mesh.shape["row"] == 1 and devices % 8 == 0:
        body = functools.partial(fused_body, devices)
    else:
        body = general_body
    return jax.shard_map(
        body,
        mesh=mesh,
        in_specs=(
            P(None, "ang", "row"),
            P(None, "row", "ang"),
            P(None, "ang", "row"),
            P(None, "row", "ang"),
        ),
        out_specs=(P(None, "row", "ang"), P(None, "row", "ang")),
        check_vma=False,
    )
```

```python
import functools

import jax
import jax.numpy as jnp
from jax import lax
from jax.experimental import pallas as pl
from jax.experimental.pallas import tpu as pltpu
from jax.sharding import PartitionSpec as P

DIMS0 = (((0,), (0,)), ((), ()))
LEVELS = 4
PLAN = (
    (
        516, 513, 514, 148, 8, 145, 146, 132888, 1541, 132614, 1576, 1174,
        1173, 1539, 34826, 2616, 34825, 34956, 68508, 34963, 35874, 69402, 35873, 3890,
        3865, 135596, 4516, 4913, 102542, 4148, 4615, 4650, 4649, 4247, 4924, 4666,
        104349, 6046, 70667, 5689, 5261, 5915, 5550, 5939, 105901, 7222, 7203, 40079,
        40765, 8095, 7221, 7723, 46910, 177583, 111671, 13883, 145830, 14757, 115519, 17831,
    ),
    (
        8, 517, 518, 792, 512, 149, 150, 552, 33801, 33802, 1168, 34360,
        33932, 34716, 34311, 1537, 1817, 100780, 2190, 2194, 35610, 2601, 2199, 2080,
        2562, 2876, 2973, 69534, 3888, 101930, 3642, 3502, 3217, 3083, 3501, 102969,
        4237, 4925, 6047, 5635, 203547, 6961, 6575, 6566, 6287, 109715, 11685, 142390,
        11317, 45611, 77858, 46113, 243518, 14130, 144807, 47159, 81467, 48163, 148287, 18227,
    ),
    (
        140, 924, 9, 10, 516, 793, 794, 428, 33934, 1172, 1577, 1578,
        1852, 1949, 1593, 34362, 1950, 34957, 35328, 34827, 2566, 35246, 2477, 2198,
        2843, 2565, 2191, 102205, 3999, 3627, 4240, 4245, 71486, 71087, 71227, 5633,
        38034, 5540, 5634, 5172, 5271, 5639, 5152, 39743, 72849, 139056, 40083, 79363,
        13365, 46897, 46134, 144806, 13733, 13345, 48162, 114482, 80951, 212787, 114723, 17831,
    ),
    (
        141, 142, 1949, 1950, 66568, 1816, 1454, 1453, 1167, 1576, 1854, 1853,
        1951, 1592, 34826, 2057, 2842, 2564, 2479, 2841, 2601, 2602, 69439, 3220,
        69177, 3083, 3642, 3584, 3589, 3590, 3222, 3867, 3221, 169515, 5264, 38459,
        103937, 5271, 5634, 5266, 5540, 5639, 5172, 171153, 39968, 40451, 144531, 13365,
        14128, 111670, 13346, 14129, 13345, 145830, 15154, 14391, 245157, 16179, 114723, 17831,
    ),
)
ORDER = (
    (
        0, 2, 1, 4, 3, 6, 5, 7, 0, 4, 1, 6,
        5, 2, 7, 3,
    ),
    (
        2, 4, 3, 0, 6, 5, 7, 1, 4, 6, 2, 0,
        3, 5, 7, 1,
    ),
    (
        4, 6, 5, 7, 2, 3, 0, 1, 4, 6, 5, 7,
        2, 0, 1, 3,
    ),
    (
        6, 7, 4, 5, 2, 3, 0, 1, 6, 7, 4, 5,
        0, 2, 1, 3,
    ),
)
OWN_AT = (8, 20, 0, 1)
L_CUTS, F_CUTS, TOP_CUTS = 1, 1, 1
DRAIN = 30
LEFT = 17


def tdot(first, second):
    return lax.dot_general(first, second, DIMS0, preferred_element_type=jnp.float32)


def split_two(value):
    high = value.astype(jnp.bfloat16)
    low = (value - high.astype(jnp.float32)).astype(jnp.bfloat16)
    return high, low


def general_body(linv_t, rhs_top, factor_t, rhs_rest):
    top_all = lax.all_gather(rhs_top, "row", axis=1, tiled=True)
    high, low = split_two(top_all)
    inverse = lax.all_gather(linv_t, "ang", axis=1, tiled=True)

    def single(first, second):
        return tdot(inverse[first], high[second]) + tdot(inverse[first], low[second])

    solved = jnp.stack([single(0, 0) - single(1, 1), single(0, 1) + single(1, 0)])
    half = lax.all_gather(solved.astype(jnp.bfloat16), "row", axis=1, tiled=True)
    factor = lax.all_gather(factor_t, "ang", axis=1, tiled=True)
    update = jnp.stack(
        [
            tdot(factor[0], half[0]) - tdot(factor[1], half[1]),
            tdot(factor[0], half[1]) + tdot(factor[1], half[0]),
        ]
    )
    return (solved, rhs_rest - update)


def fused_kernel(
    lin_ref, top_ref, fac_ref, rest_ref, acc, upd,
    glin, gfac, terms, recv, send, local,
):
    rows = lin_ref.shape[1]
    panel = lin_ref.shape[2]
    width = top_ref.shape[2]
    lane = 2 * rows
    block = 4 * rows
    blocks = panel // block
    chips = panel // lane
    wide = 2 * block
    tail = fac_ref.shape[2] // wide
    events = len(PLAN[0])
    l_kinds, f_kinds = 2 * L_CUTS, 2 * F_CUTS
    l_rows, f_rows = rows // L_CUTS, rows // F_CUTS

    me = lax.axis_index("ang")
    core = lax.rem(me, 2)
    x = lax.rem(me // 2, 2)
    y = lax.rem(me // 4, 2)
    z = me // 8
    chip = me // 2
    has_up, has_down = z < LEVELS - 1, z > 0
    targets = (
        me + 2 - 4 * x,
        me + 4 - 8 * y,
        jnp.where(has_up, me + 8, me),
        jnp.where(has_down, me - 8, me),
        me + 1 - 2 * core,
    )
    mine = pl.ds(pl.multiple_of(me * rows, rows), rows)

    def at_level(values):
        result = jnp.int32(values[0])
        for level in range(1, LEVELS):
            result = jnp.where(z == level, jnp.int32(values[level]), result)
        return result

    plan = [at_level([PLAN[level][index] for level in range(LEVELS)]) for index in range(events)]
    order = [
        at_level([ORDER[level][index] for level in range(LEVELS)]) for index in range(2 * blocks)
    ]

    def pick(words, index):
        result = words[0]
        for place in range(1, len(words)):
            result = jnp.where(index == place, words[place], result)
        return result

    own_at = at_level(OWN_AT)

    top_rows = panel // TOP_CUTS
    top_loads = [
        pltpu.make_async_copy(
            top_ref.at[:, pl.ds(cut * top_rows, top_rows), :],
            acc.at[:, pl.ds(cut * top_rows, top_rows), :],
            local.at[cut],
        )
        for cut in range(TOP_CUTS)
    ]
    loads = (
        pltpu.make_async_copy(lin_ref, glin.at[:, mine, :], local.at[TOP_CUTS]),
        pltpu.make_async_copy(fac_ref, gfac.at[:, mine, :], local.at[TOP_CUTS + 1]),
        pltpu.make_async_copy(rest_ref, upd, local.at[TOP_CUTS + 2]),
    )
    for copy in (*top_loads, *loads):
        copy.start()

    barrier = pltpu.get_barrier_semaphore()

    def greet(target):
        pl.semaphore_signal(
            barrier, inc=1, device_id={"ang": target}, device_id_type=pl.DeviceIdType.MESH
        )

    for index in (0, 1, 4):
        greet(targets[index])
    pl.when(has_up)(lambda: greet(targets[2]))
    pl.when(has_down)(lambda: greet(targets[3]))
    pl.semaphore_wait(barrier, 3 + has_up.astype(jnp.int32) + has_down.astype(jnp.int32))

    def block_at(index):
        return pl.ds(pl.multiple_of(index * block, block), block)

    def by_class(origin_chip, action):
        for quad in range(chips // 4):

            @pl.when(origin_chip // 4 == quad)
            def _(quad=quad):
                for cls in range(4 * quad, 4 * quad + 4):
                    pl.when(origin_chip == cls)(functools.partial(action, cls))

    def l_place(kind, origin, cls):
        at = pl.multiple_of(origin * rows + (kind // 2) * l_rows, l_rows)
        return glin.at[lax.rem(kind, 2), pl.ds(at, l_rows), pl.ds(cls * lane, panel - cls * lane)]

    def l_source(kind, cls):
        at = (kind // 2) * l_rows
        return lin_ref.at[kind % 2, pl.ds(at, l_rows), pl.ds(cls * lane, panel - cls * lane)]

    def f_place(kind, origin):
        at = pl.multiple_of(origin * rows + (kind // 2) * f_rows, f_rows)
        return gfac.at[lax.rem(kind, 2), pl.ds(at, f_rows), :]

    def f_source(kind):
        return fac_ref.at[kind % 2, pl.ds((kind // 2) * f_rows, f_rows), :]

    def remote(source, place, slot, origin, direction):
        return pltpu.make_async_remote_copy(
            src_ref=source,
            dst_ref=place,
            send_sem=send.at[direction, slot, origin // 2],
            recv_sem=recv.at[slot, origin],
            device_id={"ang": targets[direction]},
            device_id_type=pl.DeviceIdType.MESH,
        )

    def l_copy(kind, origin, cls, direction, own):
        source = l_source(kind, cls) if own else l_place(kind, origin, cls)
        return remote(source, l_place(jnp.int32(kind), origin, cls), kind, origin, direction)

    def f_copy(kind, origin, direction, own):
        source = f_source(kind) if own else f_place(kind, origin)
        return remote(source, f_place(jnp.int32(kind), origin), l_kinds + kind, origin, direction)

    def spread(copy_of, goes, act):
        for direction in range(5):
            copy = copy_of(direction)
            run = copy.start if act == "start" else copy.wait_send
            if goes[direction] is True:
                run()
            else:
                pl.when(goes[direction])(run)

    own_goes = (True, True, has_up, has_down, True)

    def own_l(act):
        def run(cls):
            for kind in range(l_kinds):
                spread(lambda way, kind=kind: l_copy(kind, me, cls, way, True), own_goes, act)

        by_class(chip, run)

    def own_f(act):
        for kind in range(f_kinds):
            spread(lambda way, kind=kind: f_copy(kind, me, way, True), own_goes, act)

    own_l("start")

    def split_piece(index):
        at_rows = block_at(index)
        for part in range(2):
            first, second = split_two(acc[part, at_rows, :])
            terms[pl.ds(pl.multiple_of((4 * index + 2 * part) * block, block), block), :] = first
            terms[pl.ds(pl.multiple_of((4 * index + 2 * part + 1) * block, block), block), :] = second
            acc[part, at_rows, :] = jnp.zeros((block, width), jnp.float32)

    for cut in range(TOP_CUTS):
        top_loads[cut].wait()

        @pl.loop(cut * blocks // TOP_CUTS, (cut + 1) * blocks // TOP_CUTS)
        def _(index):
            split_piece(index)

    for copy in loads:
        copy.wait()

    for index in range(blocks):
        for part in range(2):
            glin[
                part, pl.ds(index * block + lane, lane), pl.ds(index * block, lane)
            ] = jnp.zeros((lane, lane), glin.dtype)

    def solve_piece(group, index):
        at_rows, to = block_at(group), block_at(index)
        lreal, limag = glin[0, at_rows, to].T, glin[1, at_rows, to].T
        right = terms[pl.ds(pl.multiple_of(4 * group * block, block), 4 * block), :]
        real = jnp.concatenate([lreal, lreal, -limag, -limag], axis=1)
        imag = jnp.concatenate([limag, limag, lreal, lreal], axis=1)
        both = jnp.dot(
            jnp.concatenate([real, imag]), right, preferred_element_type=jnp.float32
        )
        acc[0, to, :] += both[:block]
        acc[1, to, :] += both[block:]

    def half_piece(index):
        at_rows = block_at(index)
        real = acc[0, at_rows, :].astype(jnp.bfloat16)
        imag = acc[1, at_rows, :].astype(jnp.bfloat16)
        for place, value in enumerate((-imag, real, imag)):
            to = pl.ds(pl.multiple_of((3 * index + place) * block, block), block)
            terms[to, :] = value

    def update_piece(group, index):
        at_rows, to = block_at(group), pl.ds(pl.multiple_of(index * wide, wide), wide)
        left = jnp.concatenate([gfac[1, at_rows, to].T, gfac[0, at_rows, to].T], axis=1)
        for part in range(2):
            right = terms[
                pl.ds(pl.multiple_of((3 * group + part) * block, block), 2 * block), :
            ]
            upd[part, to, :] -= jnp.dot(left, right, preferred_element_type=jnp.float32)

    def arrive_l(group):
        for side in range(2):
            origin_chip = 2 * group + side
            other = 2 * origin_chip + 1 - core

            def run(cls, other=other):
                for kind in range(l_kinds):
                    l_copy(kind, other, cls, 4, False).wait_recv()

            by_class(origin_chip, run)

    def arrive_f(group):
        for side in range(2):
            other = 2 * (2 * group + side) + 1 - core
            for kind in range(f_kinds):
                f_copy(kind, other, 4, False).wait_recv()

    def step(limit, state):
        slot, index = state
        active = slot < limit
        is_half = slot == blocks
        relative = pick(order, jnp.where(slot > blocks, slot - 1, slot))
        group = 2 * (relative // 2) + lax.rem(y + lax.rem(relative, 2), 2)

        @pl.when(jnp.logical_and(active, slot < blocks))
        def _():
            pl.when(index == 0)(lambda: arrive_l(group))
            solve_piece(group, group + index)

        @pl.when(jnp.logical_and(active, is_half))
        def _():
            half_piece(index)

        @pl.when(jnp.logical_and(active, slot > blocks))
        def _():
            pl.when(index == 0)(lambda: arrive_f(group))
            update_piece(group, index)

        size = jnp.where(slot < blocks, blocks - group, jnp.where(is_half, blocks, tail))
        done = index + 1 >= size
        next_slot = jnp.where(done, slot + 1, slot)
        next_index = jnp.where(done, 0, index + 1)
        return jnp.where(active, next_slot, slot), jnp.where(active, next_index, index)

    def decode(event):
        field = pick(plan, event)
        code = lax.rem(field, 128)
        way = lax.rem(field // 128, 8)
        kind, zo, near = code // 16, lax.rem(code // 4, 4), lax.rem(code, 4)
        xo = lax.rem(x + lax.rem(near, 2), 2)
        yo = lax.rem(y + near // 2, 2)
        same_x, same_y, same_z = lax.rem(near, 2) == 0, near // 2 == 0, z == zo
        x_first_y, x_first_z, y_first_z = way // 4 == 1, lax.rem(way // 2, 2) == 1, lax.rem(way, 2) == 1

        def implied(first, second):
            return jnp.logical_or(jnp.logical_not(first), second)

        free_x = jnp.logical_and(implied(x_first_y, same_y), implied(x_first_z, same_z))
        free_y = jnp.logical_and(jnp.logical_or(x_first_y, same_x), implied(y_first_z, same_z))
        free_z = jnp.logical_and(jnp.logical_or(x_first_z, same_x), jnp.logical_or(y_first_z, same_y))
        goes = (
            jnp.logical_and(free_x, same_x),
            jnp.logical_and(free_y, same_y),
            jnp.logical_and(free_z, jnp.logical_and(z >= zo, has_up)),
            jnp.logical_and(free_z, jnp.logical_and(z <= zo, has_down)),
            True,
        )
        origin_chip = 4 * zo + 2 * yo + xo
        return kind, origin_chip, goes, lax.rem(field // 1024, 32), field // 32768

    def run_event(event, act):
        kind, origin_chip, goes, ready, steps = decode(event)
        origin = 2 * origin_chip + core

        @pl.when(kind < l_kinds)
        def _():
            def run(cls):
                if act == "start":
                    l_copy(kind, origin, cls, 4, False).wait_recv()
                spread(lambda way: l_copy(kind, origin, cls, way, False), goes, act)

            by_class(origin_chip, run)

        @pl.when(kind >= l_kinds)
        def _():
            if act == "start":
                f_copy(kind - l_kinds, origin, 4, False).wait_recv()
            spread(lambda way: f_copy(kind - l_kinds, origin, way, False), goes, act)

        return ready, steps

    def one_event(event, state):
        pl.when(event == own_at)(lambda: own_f("start"))
        ready, steps = run_event(event, "start")

        @pl.when(event >= DRAIN)
        def _():
            run_event(event - DRAIN, "wait")

        return lax.fori_loop(0, steps, lambda _, now: step(ready, now), state)

    state = lax.fori_loop(0, events, one_event, (jnp.int32(0), jnp.int32(0)))
    slots = 2 * blocks + 1
    pieces = blocks * (blocks + 1) // 2 + blocks + blocks * tail
    lax.fori_loop(0, LEFT, lambda _, now: step(slots, now), state)

    @pl.loop(events - DRAIN, events)
    def _(event):
        run_event(event, "wait")

    own_l("wait")
    own_f("wait")


def store_kernel(acc, upd, solved_ref, updated_ref, sems):
    stores = (
        pltpu.make_async_copy(acc, solved_ref, sems.at[0]),
        pltpu.make_async_copy(upd, updated_ref, sems.at[1]),
    )
    for copy in stores:
        copy.start()
    for copy in stores:
        copy.wait()


def fused_body(devices, linv_t, rhs_top, factor_t, rhs_rest):
    parts, _, panel = linv_t.shape
    trail = rhs_rest.shape[1]
    width = rhs_top.shape[2]
    kinds = 2 * (L_CUTS + F_CUTS)
    held = pl.pallas_call(
        fused_kernel,
        out_shape=(
            pltpu.VMEM(rhs_top.shape, jnp.float32),
            pltpu.VMEM(rhs_rest.shape, jnp.float32),
        ),
        in_specs=[pl.BlockSpec(memory_space=pl.ANY)] * 4,
        out_specs=[pl.BlockSpec(memory_space=pltpu.VMEM)] * 2,
        scratch_shapes=[
            pltpu.VMEM((parts, panel, panel), linv_t.dtype),
            pltpu.VMEM((parts, panel, trail), factor_t.dtype),
            pltpu.VMEM((4 * panel, width), jnp.bfloat16),
            pltpu.SemaphoreType.DMA((kinds, devices)),
            pltpu.SemaphoreType.DMA((5, kinds, devices // 2)),
            pltpu.SemaphoreType.DMA((TOP_CUTS + 3,)),
        ],
        compiler_params=pltpu.CompilerParams(
            collective_id=0, has_side_effects=True, vmem_limit_bytes=48 << 20
        ),
    )(linv_t, rhs_top, factor_t, rhs_rest)
    return pl.pallas_call(
        store_kernel,
        out_shape=(
            jax.ShapeDtypeStruct(rhs_top.shape, jnp.float32),
            jax.ShapeDtypeStruct(rhs_rest.shape, jnp.float32),
        ),
        in_specs=[pl.BlockSpec(memory_space=pltpu.VMEM)] * 2,
        out_specs=[pl.BlockSpec(memory_space=pl.ANY)] * 2,
        scratch_shapes=[pltpu.SemaphoreType.DMA((2,))],
        compiler_params=pltpu.CompilerParams(vmem_limit_bytes=8 << 20),
    )(*(pltpu.with_memory_space_constraint(array, pltpu.VMEM) for array in held))


def solution(mesh):
    devices = mesh.shape["ang"]
    if mesh.shape["row"] == 1 and devices == 8 * LEVELS:
        body = functools.partial(fused_body, devices)
    else:
        body = general_body
    return jax.shard_map(
        body,
        mesh=mesh,
        in_specs=(
            P(None, "ang", "row"),
            P(None, "row", "ang"),
            P(None, "ang", "row"),
            P(None, "row", "ang"),
        ),
        out_specs=(P(None, "row", "ang"), P(None, "row", "ang")),
        check_vma=False,
    )
```

```python
import functools

import jax
import jax.numpy as jnp
from jax import lax
from jax.experimental import pallas as pl
from jax.experimental.pallas import tpu as pltpu
from jax.sharding import PartitionSpec as P

DIMS0 = (((0,), (0,)), ((), ()))
LEVELS = 4
PLAN = (
    (
        516, 129, 130, 532, 776, 529, 530, 66712, 1420, 1541, 1542, 66588,
        1801, 1558, 1155, 1422, 1421, 1178, 1964, 1802, 1557, 1555, 68668, 3105,
        3106, 69785, 4273, 4495, 4274, 5038, 36893, 38820, 38043, 5150, 5639, 38452,
        38667, 7085, 6179, 38973, 6679, 40879, 7347, 39967, 12350, 45608, 45621, 12854,
        242232, 12841, 13222, 12842, 12351, 179109, 14905, 48695, 15930, 81831, 48683, 15931,
    ),
    (
        776, 517, 518, 152, 128, 396, 28, 533, 534, 34569, 1802, 1552,
        67737, 2446, 2445, 2202, 35335, 34945, 2988, 2077, 2178, 2078, 2108, 3104,
        36375, 37643, 4625, 4272, 38287, 6062, 38043, 6674, 72621, 7087, 39043, 6175,
        39998, 7202, 73256, 7201, 7229, 40504, 7346, 7699, 7345, 77734, 44965, 44598,
        77365, 242218, 78394, 12841, 12323, 13223, 12351, 12855, 114233, 15915, 15539, 15931,
    ),
    (
        396, 28, 777, 778, 516, 153, 154, 397, 1422, 1053, 67614, 2988,
        2580, 35595, 2108, 2565, 2203, 2566, 2447, 2176, 4014, 35871, 4630, 37397,
        6061, 38416, 37949, 6063, 37950, 5639, 38018, 5249, 5152, 5655, 71856, 6674,
        6673, 7076, 39999, 40490, 40500, 7738, 73257, 7202, 7737, 7346, 7299, 8102,
        7699, 13221, 12321, 45622, 45233, 46635, 46645, 80443, 244771, 49063, 15927, 15539,
    ),
    (
        397, 398, 29, 30, 776, 33944, 1423, 1966, 1965, 1801, 1086, 1055,
        1085, 1802, 1540, 1178, 34969, 69551, 3851, 3135, 3604, 3589, 3590, 3227,
        3200, 70166, 4629, 4624, 4615, 5249, 71208, 5655, 105016, 6674, 6673, 72834,
        7722, 7721, 39968, 7737, 7738, 72880, 7299, 8100, 7699, 7732, 77857, 45611,
        45233, 13346, 13490, 243622, 46651, 14245, 81461, 15395, 81462, 15539, 15927, 16295,
    ),
)
ORDER = (
    (
        0, 2, 1, 4, 6, 5, 3, 7, 0, 6, 1, 7,
        2, 4, 3, 5,
    ),
    (
        2, 4, 6, 3, 0, 5, 7, 1, 6, 0, 2, 7,
        3, 4, 1, 5,
    ),
    (
        4, 6, 5, 7, 2, 3, 0, 1, 6, 7, 4, 0,
        2, 5, 3, 1,
    ),
    (
        6, 7, 4, 5, 2, 3, 0, 1, 6, 7, 4, 0,
        5, 2, 1, 3,
    ),
)
OWN_AT = (8, 30, 30, 2)
L_CUTS, F_CUTS, TOP_CUTS = 1, 1, 1
DRAIN = 30
LEFT = 4
LATE = 2
STORE_CUTS = 2


def tdot(first, second):
    return lax.dot_general(first, second, DIMS0, preferred_element_type=jnp.float32)


def split_two(value):
    high = value.astype(jnp.bfloat16)
    low = (value - high.astype(jnp.float32)).astype(jnp.bfloat16)
    return high, low


def general_body(linv_t, rhs_top, factor_t, rhs_rest):
    top_all = lax.all_gather(rhs_top, "row", axis=1, tiled=True)
    high, low = split_two(top_all)
    inverse = lax.all_gather(linv_t, "ang", axis=1, tiled=True)

    def single(first, second):
        return tdot(inverse[first], high[second]) + tdot(inverse[first], low[second])

    solved = jnp.stack([single(0, 0) - single(1, 1), single(0, 1) + single(1, 0)])
    half = lax.all_gather(solved.astype(jnp.bfloat16), "row", axis=1, tiled=True)
    factor = lax.all_gather(factor_t, "ang", axis=1, tiled=True)
    update = jnp.stack(
        [
            tdot(factor[0], half[0]) - tdot(factor[1], half[1]),
            tdot(factor[0], half[1]) + tdot(factor[1], half[0]),
        ]
    )
    return (solved, rhs_rest - update)


def group_of(relative, y):
    return 2 * (relative // 2) + lax.rem(y + lax.rem(relative, 2), 2)


def update_piece(gfac, terms, upd, groups, block, start, size):
    to = pl.ds(start, size)
    lefts, rights = [], [[], []]
    for group in groups:
        at_rows = pl.ds(pl.multiple_of(group * block, block), block)
        lefts += [gfac[1, at_rows, to].T, gfac[0, at_rows, to].T]
        for part in range(2):
            at_terms = pl.ds(pl.multiple_of((3 * group + part) * block, block), 2 * block)
            rights[part].append(terms[at_terms, :])
    left = jnp.concatenate(lefts, axis=1)
    for part in range(2):
        right = jnp.concatenate(rights[part])
        upd[part, to, :] -= jnp.dot(left, right, preferred_element_type=jnp.float32)


def fused_kernel(
    lin_ref, top_ref, fac_ref, rest_ref, acc, upd, gfac, terms,
    glin, recv, send, local,
):
    rows = lin_ref.shape[1]
    panel = lin_ref.shape[2]
    width = top_ref.shape[2]
    lane = 2 * rows
    block = 4 * rows
    blocks = panel // block
    chips = panel // lane
    events = len(PLAN[0])
    l_kinds, f_kinds = 2 * L_CUTS, 2 * F_CUTS
    l_rows, f_rows = rows // L_CUTS, rows // F_CUTS

    me = lax.axis_index("ang")
    core = lax.rem(me, 2)
    x = lax.rem(me // 2, 2)
    y = lax.rem(me // 4, 2)
    z = me // 8
    chip = me // 2
    has_up, has_down = z < LEVELS - 1, z > 0
    targets = (
        me + 2 - 4 * x,
        me + 4 - 8 * y,
        jnp.where(has_up, me + 8, me),
        jnp.where(has_down, me - 8, me),
        me + 1 - 2 * core,
    )
    mine = pl.ds(pl.multiple_of(me * rows, rows), rows)

    def at_level(values):
        result = jnp.int32(values[0])
        for level in range(1, LEVELS):
            result = jnp.where(z == level, jnp.int32(values[level]), result)
        return result

    plan = [at_level([PLAN[level][index] for level in range(LEVELS)]) for index in range(events)]
    order = [
        at_level([ORDER[level][index] for level in range(LEVELS)]) for index in range(2 * blocks)
    ]

    def pick(words, index):
        result = words[0]
        for place in range(1, len(words)):
            result = jnp.where(index == place, words[place], result)
        return result

    own_at = at_level(OWN_AT)

    top_rows = panel // TOP_CUTS
    top_loads = [
        pltpu.make_async_copy(
            top_ref.at[:, pl.ds(cut * top_rows, top_rows), :],
            acc.at[:, pl.ds(cut * top_rows, top_rows), :],
            local.at[cut],
        )
        for cut in range(TOP_CUTS)
    ]
    loads = (
        pltpu.make_async_copy(lin_ref, glin.at[:, mine, :], local.at[TOP_CUTS]),
        pltpu.make_async_copy(fac_ref, gfac.at[:, mine, :], local.at[TOP_CUTS + 1]),
        pltpu.make_async_copy(rest_ref, upd, local.at[TOP_CUTS + 2]),
    )
    for copy in (*top_loads, *loads):
        copy.start()

    barrier = pltpu.get_barrier_semaphore()

    def greet(target):
        pl.semaphore_signal(
            barrier, inc=1, device_id={"ang": target}, device_id_type=pl.DeviceIdType.MESH
        )

    for index in (0, 1, 4):
        greet(targets[index])
    pl.when(has_up)(lambda: greet(targets[2]))
    pl.when(has_down)(lambda: greet(targets[3]))
    pl.semaphore_wait(barrier, 3 + has_up.astype(jnp.int32) + has_down.astype(jnp.int32))

    def block_at(index):
        return pl.ds(pl.multiple_of(index * block, block), block)

    def by_class(origin_chip, action):
        for quad in range(chips // 4):

            @pl.when(origin_chip // 4 == quad)
            def _(quad=quad):
                for cls in range(4 * quad, 4 * quad + 4):
                    pl.when(origin_chip == cls)(functools.partial(action, cls))

    def l_place(kind, origin, cls):
        at = pl.multiple_of(origin * rows + (kind // 2) * l_rows, l_rows)
        return glin.at[lax.rem(kind, 2), pl.ds(at, l_rows), pl.ds(cls * lane, panel - cls * lane)]

    def l_source(kind, cls):
        at = (kind // 2) * l_rows
        return lin_ref.at[kind % 2, pl.ds(at, l_rows), pl.ds(cls * lane, panel - cls * lane)]

    def f_place(kind, origin):
        at = pl.multiple_of(origin * rows + (kind // 2) * f_rows, f_rows)
        return gfac.at[lax.rem(kind, 2), pl.ds(at, f_rows), :]

    def f_source(kind):
        return fac_ref.at[kind % 2, pl.ds((kind // 2) * f_rows, f_rows), :]

    def remote(source, place, slot, origin, direction):
        return pltpu.make_async_remote_copy(
            src_ref=source,
            dst_ref=place,
            send_sem=send.at[direction, slot, origin // 2],
            recv_sem=recv.at[slot, origin],
            device_id={"ang": targets[direction]},
            device_id_type=pl.DeviceIdType.MESH,
        )

    def l_copy(kind, origin, cls, direction, own):
        source = l_source(kind, cls) if own else l_place(kind, origin, cls)
        return remote(source, l_place(jnp.int32(kind), origin, cls), kind, origin, direction)

    def f_copy(kind, origin, direction, own):
        source = f_source(kind) if own else f_place(kind, origin)
        return remote(source, f_place(jnp.int32(kind), origin), l_kinds + kind, origin, direction)

    def spread(copy_of, goes, act):
        for direction in range(5):
            copy = copy_of(direction)
            run = copy.start if act == "start" else copy.wait_send
            if goes[direction] is True:
                run()
            else:
                pl.when(goes[direction])(run)

    own_goes = (True, True, has_up, has_down, True)

    def own_l(act):
        def run(cls):
            for kind in range(l_kinds):
                spread(lambda way, kind=kind: l_copy(kind, me, cls, way, True), own_goes, act)

        by_class(chip, run)

    def own_f(act):
        for kind in range(f_kinds):
            spread(lambda way, kind=kind: f_copy(kind, me, way, True), own_goes, act)

    own_l("start")

    def split_piece(index):
        at_rows = block_at(index)
        for part in range(2):
            first, second = split_two(acc[part, at_rows, :])
            terms[pl.ds(pl.multiple_of((4 * index + 2 * part) * block, block), block), :] = first
            terms[pl.ds(pl.multiple_of((4 * index + 2 * part + 1) * block, block), block), :] = second
            acc[part, at_rows, :] = jnp.zeros((block, width), jnp.float32)

    for cut in range(TOP_CUTS):
        top_loads[cut].wait()

        @pl.loop(cut * blocks // TOP_CUTS, (cut + 1) * blocks // TOP_CUTS)
        def _(index):
            split_piece(index)

    for copy in loads:
        copy.wait()

    for index in range(blocks):
        for part in range(2):
            glin[
                part, pl.ds(index * block + lane, lane), pl.ds(index * block, lane)
            ] = jnp.zeros((lane, lane), glin.dtype)

    def solve_piece(group, index, count):
        size = count * block
        at_rows, to = block_at(group), pl.ds(pl.multiple_of(index * block, block), size)
        lreal, limag = glin[0, at_rows, to].T, glin[1, at_rows, to].T
        right = terms[pl.ds(pl.multiple_of(4 * group * block, block), 4 * block), :]
        real = jnp.concatenate([lreal, lreal, -limag, -limag], axis=1)
        imag = jnp.concatenate([limag, limag, lreal, lreal], axis=1)
        both = jnp.dot(
            jnp.concatenate([real, imag]), right, preferred_element_type=jnp.float32
        )
        acc[0, to, :] += both[:size]
        acc[1, to, :] += both[size:]

    def half_piece(index):
        at_rows = block_at(index)
        real = acc[0, at_rows, :].astype(jnp.bfloat16)
        imag = acc[1, at_rows, :].astype(jnp.bfloat16)
        for place, value in enumerate((-imag, real, imag)):
            to = pl.ds(pl.multiple_of((3 * index + place) * block, block), block)
            terms[to, :] = value

    def arrive_l(group):
        for side in range(2):
            origin_chip = 2 * group + side
            other = 2 * origin_chip + 1 - core

            def run(cls, other=other):
                for kind in range(l_kinds):
                    l_copy(kind, other, cls, 4, False).wait_recv()

            by_class(origin_chip, run)

    def arrive_f(group):
        for side in range(2):
            other = 2 * (2 * group + side) + 1 - core
            for kind in range(f_kinds):
                f_copy(kind, other, 4, False).wait_recv()

    def step(limit, state):
        slot, index = state
        active = slot < limit
        is_half = slot == blocks
        relative = pick(order, jnp.where(slot > blocks, slot - 1, slot))
        group = group_of(relative, y)

        @pl.when(jnp.logical_and(active, slot < blocks))
        def _():
            pl.when(index == 0)(lambda: arrive_l(group))
            first = group + 2 * index
            pl.when(first + 1 < blocks)(lambda: solve_piece(group, first, 2))
            pl.when(first + 1 == blocks)(lambda: solve_piece(group, first, 1))

        @pl.when(jnp.logical_and(active, is_half))
        def _():
            half_piece(index)

        @pl.when(jnp.logical_and(active, slot > blocks))
        def _():
            arrive_f(group)
            update_piece(gfac, terms, upd, (group,), block, 0, fac_ref.shape[2])

        size = jnp.where(slot < blocks, (blocks - group + 1) // 2, jnp.where(is_half, blocks, 1))
        done = index + 1 >= size
        next_slot = jnp.where(done, slot + 1, slot)
        next_index = jnp.where(done, 0, index + 1)
        return jnp.where(active, next_slot, slot), jnp.where(active, next_index, index)

    def decode(event):
        field = pick(plan, event)
        code = lax.rem(field, 128)
        way = lax.rem(field // 128, 8)
        kind, zo, near = code // 16, lax.rem(code // 4, 4), lax.rem(code, 4)
        xo = lax.rem(x + lax.rem(near, 2), 2)
        yo = lax.rem(y + near // 2, 2)
        same_x, same_y, same_z = lax.rem(near, 2) == 0, near // 2 == 0, z == zo
        x_first_y, x_first_z, y_first_z = way // 4 == 1, lax.rem(way // 2, 2) == 1, lax.rem(way, 2) == 1

        def implied(first, second):
            return jnp.logical_or(jnp.logical_not(first), second)

        free_x = jnp.logical_and(implied(x_first_y, same_y), implied(x_first_z, same_z))
        free_y = jnp.logical_and(jnp.logical_or(x_first_y, same_x), implied(y_first_z, same_z))
        free_z = jnp.logical_and(jnp.logical_or(x_first_z, same_x), jnp.logical_or(y_first_z, same_y))
        goes = (
            jnp.logical_and(free_x, same_x),
            jnp.logical_and(free_y, same_y),
            jnp.logical_and(free_z, jnp.logical_and(z >= zo, has_up)),
            jnp.logical_and(free_z, jnp.logical_and(z <= zo, has_down)),
            True,
        )
        origin_chip = 4 * zo + 2 * yo + xo
        return kind, origin_chip, goes, lax.rem(field // 1024, 32), field // 32768

    def run_event(event, act):
        kind, origin_chip, goes, ready, steps = decode(event)
        origin = 2 * origin_chip + core

        @pl.when(kind < l_kinds)
        def _():
            def run(cls):
                if act == "start":
                    l_copy(kind, origin, cls, 4, False).wait_recv()
                spread(lambda way: l_copy(kind, origin, cls, way, False), goes, act)

            by_class(origin_chip, run)

        @pl.when(kind >= l_kinds)
        def _():
            if act == "start":
                f_copy(kind - l_kinds, origin, 4, False).wait_recv()
            spread(lambda way: f_copy(kind - l_kinds, origin, way, False), goes, act)

        return ready, steps

    def one_event(event, state):
        pl.when(event == own_at)(lambda: own_f("start"))
        ready, steps = run_event(event, "start")

        @pl.when(event >= DRAIN)
        def _():
            run_event(event - DRAIN, "wait")

        return lax.fori_loop(0, steps, lambda _, now: step(ready, now), state)

    state = lax.fori_loop(0, events, one_event, (jnp.int32(0), jnp.int32(0)))
    slots = 2 * blocks + 1 - LATE
    lax.fori_loop(0, LEFT, lambda _, now: step(slots, now), state)

    @pl.loop(events - DRAIN, events)
    def _(event):
        run_event(event, "wait")

    for place in range(2 * blocks - LATE, 2 * blocks):
        arrive_f(group_of(order[place], y))
    own_l("wait")
    own_f("wait")


def store_kernel(acc, upd, gfac, terms, solved_ref, updated_ref, rest, sems):
    me = lax.axis_index("ang")
    y = lax.rem(me // 4, 2)
    z = me // 8
    trail = gfac.shape[2]
    block = gfac.shape[1] // (len(ORDER[0]) // 2)
    size = trail // STORE_CUTS
    groups = []
    for place in range(len(ORDER[0]) - LATE, len(ORDER[0])):
        relative = jnp.int32(ORDER[0][place])
        for level in range(1, LEVELS):
            relative = jnp.where(z == level, jnp.int32(ORDER[level][place]), relative)
        groups.append(group_of(relative, y))
    stores = [pltpu.make_async_copy(acc, solved_ref, sems.at[0])]
    stores[0].start()
    for cut in range(STORE_CUTS):
        at = pl.ds(cut * size, size)
        rest[:, at, :] = upd[:, at, :]
        update_piece(gfac, terms, rest, groups, block, cut * size, size)
        stores.append(
            pltpu.make_async_copy(
                rest.at[:, at, :], updated_ref.at[:, at, :], sems.at[1 + cut]
            )
        )
        stores[-1].start()
    for copy in stores:
        copy.wait()


def fused_body(devices, linv_t, rhs_top, factor_t, rhs_rest):
    parts, _, panel = linv_t.shape
    trail = rhs_rest.shape[1]
    width = rhs_top.shape[2]
    kinds = 2 * (L_CUTS + F_CUTS)
    held = pl.pallas_call(
        fused_kernel,
        out_shape=(
            pltpu.VMEM(rhs_top.shape, jnp.float32),
            pltpu.VMEM(rhs_rest.shape, jnp.float32),
            pltpu.VMEM((parts, panel, trail), factor_t.dtype),
            pltpu.VMEM((4 * panel, width), jnp.bfloat16),
        ),
        in_specs=[pl.BlockSpec(memory_space=pl.ANY)] * 4,
        out_specs=[pl.BlockSpec(memory_space=pltpu.VMEM)] * 4,
        scratch_shapes=[
            pltpu.VMEM((parts, panel, panel), linv_t.dtype),
            pltpu.SemaphoreType.DMA((kinds, devices)),
            pltpu.SemaphoreType.DMA((5, kinds, devices // 2)),
            pltpu.SemaphoreType.DMA((TOP_CUTS + 3,)),
        ],
        compiler_params=pltpu.CompilerParams(
            collective_id=0, has_side_effects=True, vmem_limit_bytes=30 << 20
        ),
    )(linv_t, rhs_top, factor_t, rhs_rest)
    return pl.pallas_call(
        store_kernel,
        out_shape=(
            jax.ShapeDtypeStruct(rhs_top.shape, jnp.float32),
            jax.ShapeDtypeStruct(rhs_rest.shape, jnp.float32),
        ),
        in_specs=[pl.BlockSpec(memory_space=pltpu.VMEM)] * 4,
        out_specs=[pl.BlockSpec(memory_space=pl.ANY)] * 2,
        scratch_shapes=[
            pltpu.VMEM(rhs_rest.shape, jnp.float32),
            pltpu.SemaphoreType.DMA((1 + STORE_CUTS,)),
        ],
        compiler_params=pltpu.CompilerParams(vmem_limit_bytes=30 << 20),
    )(*(pltpu.with_memory_space_constraint(array, pltpu.VMEM) for array in held))


def solution(mesh):
    devices = mesh.shape["ang"]
    if mesh.shape["row"] == 1 and devices == 8 * LEVELS:
        body = functools.partial(fused_body, devices)
    else:
        body = general_body
    return jax.shard_map(
        body,
        mesh=mesh,
        in_specs=(
            P(None, "ang", "row"),
            P(None, "row", "ang"),
            P(None, "ang", "row"),
            P(None, "row", "ang"),
        ),
        out_specs=(P(None, "row", "ang"), P(None, "row", "ang")),
        check_vma=False,
    )
```

```python
import functools

import jax
import jax.numpy as jnp
from jax import lax
from jax.experimental import pallas as pl
from jax.experimental.pallas import tpu as pltpu
from jax.sharding import PartitionSpec as P

DIMS0 = (((0,), (0,)), ((), ()))
LEVELS = 4
PLAN = (
    (
        516, 129, 130, 532, 776, 529, 530, 33944, 34188, 1541, 1542, 33820,
        34569, 1558, 1155, 1422, 1421, 1178, 1964, 1802, 1557, 1555, 68668, 3105,
        3106, 69785, 4273, 4495, 4274, 5038, 36893, 38820, 38043, 5150, 5639, 38452,
        38667, 6061, 6179, 71741, 6679, 7087, 40115, 7199, 39998, 45608, 12853, 12854,
        242232, 12841, 13222, 12842, 12351, 179109, 14905, 14903, 14906, 81831, 81451, 15931,
    ),
    (
        776, 517, 518, 152, 128, 396, 28, 533, 534, 777, 34570, 1552,
        67737, 2446, 2445, 2202, 35335, 34945, 2988, 2077, 2178, 2078, 3132, 3104,
        36375, 3851, 4625, 4272, 71055, 6062, 71835, 6674, 72621, 7087, 6275, 6175,
        38974, 7202, 106024, 7201, 7229, 7736, 7346, 7699, 7345, 77734, 44965, 44598,
        110133, 209450, 78394, 12841, 12323, 13223, 12351, 12855, 114233, 15915, 15539, 15931,
    ),
    (
        396, 28, 777, 778, 516, 153, 154, 397, 398, 29, 30, 35756,
        35348, 35595, 2108, 2565, 2203, 2566, 2447, 2176, 4014, 69663, 37398, 4629,
        5037, 4624, 4157, 5039, 103486, 5639, 5250, 5249, 5152, 5655, 104624, 6674,
        6673, 7076, 6207, 6698, 106036, 7738, 40489, 7202, 7737, 7346, 7299, 8102,
        7699, 13221, 45089, 45622, 45233, 46635, 177717, 147003, 80931, 49063, 15927, 15539,
    ),
    (
        397, 398, 29, 30, 776, 1176, 34191, 1966, 1965, 1801, 1086, 1055,
        1085, 1802, 1540, 34970, 2201, 2991, 3851, 3135, 69140, 3589, 3590, 3227,
        3200, 70166, 4629, 4624, 4615, 5249, 38440, 38423, 105016, 6674, 6673, 39042,
        7722, 40489, 7200, 40505, 40506, 40112, 7299, 8100, 7699, 7732, 45089, 78379,
        12465, 12322, 46258, 243622, 80443, 15269, 47669, 15395, 81462, 48307, 15927, 16295,
    ),
)
ORDER = (
    (
        0, 2, 1, 4, 6, 5, 3, 7, 0, 6, 1, 7,
        2, 4, 3, 5,
    ),
    (
        2, 4, 6, 3, 0, 5, 7, 1, 6, 0, 2, 7,
        3, 4, 1, 5,
    ),
    (
        4, 6, 5, 7, 2, 3, 0, 1, 6, 7, 4, 0,
        2, 5, 3, 1,
    ),
    (
        6, 7, 4, 5, 2, 3, 0, 1, 6, 7, 4, 0,
        5, 2, 1, 3,
    ),
)
OWN_AT = (8, 30, 30, 2)
L_CUTS, F_CUTS, TOP_CUTS = 1, 1, 4
DRAIN = 30
LEFT = 2
LATE = 2
STORE_CUTS = 2


def tdot(first, second):
    return lax.dot_general(first, second, DIMS0, preferred_element_type=jnp.float32)


def split_two(value):
    high = value.astype(jnp.bfloat16)
    low = (value - high.astype(jnp.float32)).astype(jnp.bfloat16)
    return high, low


def general_body(linv_t, rhs_top, factor_t, rhs_rest):
    top_all = lax.all_gather(rhs_top, "row", axis=1, tiled=True)
    high, low = split_two(top_all)
    inverse = lax.all_gather(linv_t, "ang", axis=1, tiled=True)

    def single(first, second):
        return tdot(inverse[first], high[second]) + tdot(inverse[first], low[second])

    solved = jnp.stack([single(0, 0) - single(1, 1), single(0, 1) + single(1, 0)])
    half = lax.all_gather(solved.astype(jnp.bfloat16), "row", axis=1, tiled=True)
    factor = lax.all_gather(factor_t, "ang", axis=1, tiled=True)
    update = jnp.stack(
        [
            tdot(factor[0], half[0]) - tdot(factor[1], half[1]),
            tdot(factor[0], half[1]) + tdot(factor[1], half[0]),
        ]
    )
    return (solved, rhs_rest - update)


def group_of(relative, y):
    return 2 * (relative // 2) + lax.rem(y + lax.rem(relative, 2), 2)


def update_piece(gfac, terms, upd, groups, block, start, size):
    to = pl.ds(start, size)
    lefts, rights = [], [[], []]
    for group in groups:
        at_rows = pl.ds(pl.multiple_of(group * block, block), block)
        lefts += [gfac[1, at_rows, to].T, gfac[0, at_rows, to].T]
        for part in range(2):
            at_terms = pl.ds(pl.multiple_of((3 * group + part) * block, block), 2 * block)
            rights[part].append(terms[at_terms, :])
    left = jnp.concatenate(lefts, axis=1)
    for part in range(2):
        right = jnp.concatenate(rights[part])
        upd[part, to, :] -= jnp.dot(left, right, preferred_element_type=jnp.float32)


def fused_kernel(
    lin_ref, top_ref, fac_ref, rest_ref, acc, upd, gfac, terms,
    glin, recv, send, local,
):
    rows = lin_ref.shape[1]
    panel = lin_ref.shape[2]
    width = top_ref.shape[2]
    lane = 2 * rows
    block = 4 * rows
    blocks = panel // block
    chips = panel // lane
    events = len(PLAN[0])
    l_kinds, f_kinds = 2 * L_CUTS, 2 * F_CUTS
    l_rows, f_rows = rows // L_CUTS, rows // F_CUTS

    me = lax.axis_index("ang")
    core = lax.rem(me, 2)
    x = lax.rem(me // 2, 2)
    y = lax.rem(me // 4, 2)
    z = me // 8
    chip = me // 2
    has_up, has_down = z < LEVELS - 1, z > 0
    targets = (
        me + 2 - 4 * x,
        me + 4 - 8 * y,
        jnp.where(has_up, me + 8, me),
        jnp.where(has_down, me - 8, me),
        me + 1 - 2 * core,
    )
    mine = pl.ds(pl.multiple_of(me * rows, rows), rows)

    def at_level(values):
        result = jnp.int32(values[0])
        for level in range(1, LEVELS):
            result = jnp.where(z == level, jnp.int32(values[level]), result)
        return result

    plan = [at_level([PLAN[level][index] for level in range(LEVELS)]) for index in range(events)]
    order = [
        at_level([ORDER[level][index] for level in range(LEVELS)]) for index in range(2 * blocks)
    ]

    def pick(words, index):
        result = words[0]
        for place in range(1, len(words)):
            result = jnp.where(index == place, words[place], result)
        return result

    own_at = at_level(OWN_AT)

    top_rows = panel // TOP_CUTS
    top_loads = [
        pltpu.make_async_copy(
            top_ref.at[:, pl.ds(cut * top_rows, top_rows), :],
            acc.at[:, pl.ds(cut * top_rows, top_rows), :],
            local.at[cut],
        )
        for cut in range(TOP_CUTS)
    ]
    loads = (
        pltpu.make_async_copy(lin_ref, glin.at[:, mine, :], local.at[TOP_CUTS]),
        pltpu.make_async_copy(fac_ref, gfac.at[:, mine, :], local.at[TOP_CUTS + 1]),
        pltpu.make_async_copy(rest_ref, upd, local.at[TOP_CUTS + 2]),
    )
    for copy in (*top_loads, *loads):
        copy.start()

    barrier = pltpu.get_barrier_semaphore()

    def greet(target):
        pl.semaphore_signal(
            barrier, inc=1, device_id={"ang": target}, device_id_type=pl.DeviceIdType.MESH
        )

    for index in (0, 1, 4):
        greet(targets[index])
    pl.when(has_up)(lambda: greet(targets[2]))
    pl.when(has_down)(lambda: greet(targets[3]))
    pl.semaphore_wait(barrier, 3 + has_up.astype(jnp.int32) + has_down.astype(jnp.int32))

    def block_at(index):
        return pl.ds(pl.multiple_of(index * block, block), block)

    def by_class(origin_chip, action):
        for quad in range(chips // 4):

            @pl.when(origin_chip // 4 == quad)
            def _(quad=quad):
                for cls in range(4 * quad, 4 * quad + 4):
                    pl.when(origin_chip == cls)(functools.partial(action, cls))

    def l_place(kind, origin, cls):
        at = pl.multiple_of(origin * rows + (kind // 2) * l_rows, l_rows)
        return glin.at[lax.rem(kind, 2), pl.ds(at, l_rows), pl.ds(cls * lane, panel - cls * lane)]

    def l_source(kind, cls):
        at = (kind // 2) * l_rows
        return lin_ref.at[kind % 2, pl.ds(at, l_rows), pl.ds(cls * lane, panel - cls * lane)]

    def f_place(kind, origin):
        at = pl.multiple_of(origin * rows + (kind // 2) * f_rows, f_rows)
        return gfac.at[lax.rem(kind, 2), pl.ds(at, f_rows), :]

    def f_source(kind):
        return fac_ref.at[kind % 2, pl.ds((kind // 2) * f_rows, f_rows), :]

    def remote(source, place, slot, origin, direction):
        return pltpu.make_async_remote_copy(
            src_ref=source,
            dst_ref=place,
            send_sem=send.at[direction, slot, origin // 2],
            recv_sem=recv.at[slot, origin],
            device_id={"ang": targets[direction]},
            device_id_type=pl.DeviceIdType.MESH,
        )

    def l_copy(kind, origin, cls, direction, own):
        source = l_source(kind, cls) if own else l_place(kind, origin, cls)
        return remote(source, l_place(jnp.int32(kind), origin, cls), kind, origin, direction)

    def f_copy(kind, origin, direction, own):
        source = f_source(kind) if own else f_place(kind, origin)
        return remote(source, f_place(jnp.int32(kind), origin), l_kinds + kind, origin, direction)

    def spread(copy_of, goes, act):
        for direction in range(5):
            copy = copy_of(direction)
            run = copy.start if act == "start" else copy.wait_send
            if goes[direction] is True:
                run()
            else:
                pl.when(goes[direction])(run)

    own_goes = (True, True, has_up, has_down, True)

    def own_l(act):
        def run(cls):
            for kind in range(l_kinds):
                spread(lambda way, kind=kind: l_copy(kind, me, cls, way, True), own_goes, act)

        by_class(chip, run)

    def own_f(act):
        for kind in range(f_kinds):
            spread(lambda way, kind=kind: f_copy(kind, me, way, True), own_goes, act)

    own_l("start")

    def split_piece(index):
        at_rows = block_at(index)
        for part in range(2):
            first, second = split_two(acc[part, at_rows, :])
            terms[pl.ds(pl.multiple_of((4 * index + 2 * part) * block, block), block), :] = first
            terms[pl.ds(pl.multiple_of((4 * index + 2 * part + 1) * block, block), block), :] = second
            acc[part, at_rows, :] = jnp.zeros((block, width), jnp.float32)

    for cut in range(TOP_CUTS):
        top_loads[cut].wait()

        @pl.loop(cut * blocks // TOP_CUTS, (cut + 1) * blocks // TOP_CUTS)
        def _(index):
            split_piece(index)

    for copy in loads:
        copy.wait()

    for index in range(blocks):
        for part in range(2):
            glin[
                part, pl.ds(index * block + lane, lane), pl.ds(index * block, lane)
            ] = jnp.zeros((lane, lane), glin.dtype)

    def solve_piece(group, index, count):
        size = count * block
        at_rows, to = block_at(group), pl.ds(pl.multiple_of(index * block, block), size)
        lreal, limag = glin[0, at_rows, to].T, glin[1, at_rows, to].T
        right = terms[pl.ds(pl.multiple_of(4 * group * block, block), 4 * block), :]
        real = jnp.concatenate([lreal, lreal, -limag, -limag], axis=1)
        imag = jnp.concatenate([limag, limag, lreal, lreal], axis=1)
        both = jnp.dot(
            jnp.concatenate([real, imag]), right, preferred_element_type=jnp.float32
        )
        acc[0, to, :] += both[:size]
        acc[1, to, :] += both[size:]

    def half_piece(index):
        at_rows = block_at(index)
        real = acc[0, at_rows, :].astype(jnp.bfloat16)
        imag = acc[1, at_rows, :].astype(jnp.bfloat16)
        for place, value in enumerate((-imag, real, imag)):
            to = pl.ds(pl.multiple_of((3 * index + place) * block, block), block)
            terms[to, :] = value

    def arrive_l(group):
        for side in range(2):
            origin_chip = 2 * group + side
            other = 2 * origin_chip + 1 - core

            def run(cls, other=other):
                for kind in range(l_kinds):
                    l_copy(kind, other, cls, 4, False).wait_recv()

            by_class(origin_chip, run)

    def arrive_f(group):
        for side in range(2):
            other = 2 * (2 * group + side) + 1 - core
            for kind in range(f_kinds):
                f_copy(kind, other, 4, False).wait_recv()

    def step(limit, state):
        slot, index = state
        active = slot < limit
        is_half = slot == blocks
        relative = pick(order, jnp.where(slot > blocks, slot - 1, slot))
        group = group_of(relative, y)

        @pl.when(jnp.logical_and(active, slot < blocks))
        def _():
            pl.when(index == 0)(lambda: arrive_l(group))
            first = group + 2 * index
            pl.when(first + 1 < blocks)(lambda: solve_piece(group, first, 2))
            pl.when(first + 1 == blocks)(lambda: solve_piece(group, first, 1))

        @pl.when(jnp.logical_and(active, is_half))
        def _():
            half_piece(index)

        @pl.when(jnp.logical_and(active, slot > blocks))
        def _():
            arrive_f(group)
            update_piece(gfac, terms, upd, (group,), block, 0, fac_ref.shape[2])

        size = jnp.where(slot < blocks, (blocks - group + 1) // 2, jnp.where(is_half, blocks, 1))
        done = index + 1 >= size
        next_slot = jnp.where(done, slot + 1, slot)
        next_index = jnp.where(done, 0, index + 1)
        return jnp.where(active, next_slot, slot), jnp.where(active, next_index, index)

    def decode(event):
        field = pick(plan, event)
        code = lax.rem(field, 128)
        way = lax.rem(field // 128, 8)
        kind, zo, near = code // 16, lax.rem(code // 4, 4), lax.rem(code, 4)
        xo = lax.rem(x + lax.rem(near, 2), 2)
        yo = lax.rem(y + near // 2, 2)
        same_x, same_y, same_z = lax.rem(near, 2) == 0, near // 2 == 0, z == zo
        x_first_y, x_first_z, y_first_z = way // 4 == 1, lax.rem(way // 2, 2) == 1, lax.rem(way, 2) == 1

        def implied(first, second):
            return jnp.logical_or(jnp.logical_not(first), second)

        free_x = jnp.logical_and(implied(x_first_y, same_y), implied(x_first_z, same_z))
        free_y = jnp.logical_and(jnp.logical_or(x_first_y, same_x), implied(y_first_z, same_z))
        free_z = jnp.logical_and(jnp.logical_or(x_first_z, same_x), jnp.logical_or(y_first_z, same_y))
        goes = (
            jnp.logical_and(free_x, same_x),
            jnp.logical_and(free_y, same_y),
            jnp.logical_and(free_z, jnp.logical_and(z >= zo, has_up)),
            jnp.logical_and(free_z, jnp.logical_and(z <= zo, has_down)),
            True,
        )
        origin_chip = 4 * zo + 2 * yo + xo
        return kind, origin_chip, goes, lax.rem(field // 1024, 32), field // 32768

    def run_event(event, act):
        kind, origin_chip, goes, ready, steps = decode(event)
        origin = 2 * origin_chip + core

        @pl.when(kind < l_kinds)
        def _():
            def run(cls):
                if act == "start":
                    l_copy(kind, origin, cls, 4, False).wait_recv()
                spread(lambda way: l_copy(kind, origin, cls, way, False), goes, act)

            by_class(origin_chip, run)

        @pl.when(kind >= l_kinds)
        def _():
            if act == "start":
                f_copy(kind - l_kinds, origin, 4, False).wait_recv()
            spread(lambda way: f_copy(kind - l_kinds, origin, way, False), goes, act)

        return ready, steps

    def one_event(event, state):
        pl.when(event == own_at)(lambda: own_f("start"))
        ready, steps = run_event(event, "start")

        @pl.when(event >= DRAIN)
        def _():
            run_event(event - DRAIN, "wait")

        return lax.fori_loop(0, steps, lambda _, now: step(ready, now), state)

    state = lax.fori_loop(0, events, one_event, (jnp.int32(0), jnp.int32(0)))
    slots = 2 * blocks + 1 - LATE
    lax.fori_loop(0, LEFT, lambda _, now: step(slots, now), state)

    @pl.loop(events - DRAIN, events)
    def _(event):
        run_event(event, "wait")

    for place in range(2 * blocks - LATE, 2 * blocks):
        arrive_f(group_of(order[place], y))
    own_l("wait")
    own_f("wait")


def store_kernel(acc, upd, gfac, terms, solved_ref, updated_ref, rest, sems):
    me = lax.axis_index("ang")
    y = lax.rem(me // 4, 2)
    z = me // 8
    trail = gfac.shape[2]
    block = gfac.shape[1] // (len(ORDER[0]) // 2)
    size = trail // STORE_CUTS
    groups = []
    for place in range(len(ORDER[0]) - LATE, len(ORDER[0])):
        relative = jnp.int32(ORDER[0][place])
        for level in range(1, LEVELS):
            relative = jnp.where(z == level, jnp.int32(ORDER[level][place]), relative)
        groups.append(group_of(relative, y))
    stores = [pltpu.make_async_copy(acc, solved_ref, sems.at[0])]
    stores[0].start()
    for cut in range(STORE_CUTS):
        at = pl.ds(cut * size, size)
        rest[:, at, :] = upd[:, at, :]
        update_piece(gfac, terms, rest, groups, block, cut * size, size)
        stores.append(
            pltpu.make_async_copy(
                rest.at[:, at, :], updated_ref.at[:, at, :], sems.at[1 + cut]
            )
        )
        stores[-1].start()
    for copy in stores:
        copy.wait()


def fused_body(devices, linv_t, rhs_top, factor_t, rhs_rest):
    parts, _, panel = linv_t.shape
    trail = rhs_rest.shape[1]
    width = rhs_top.shape[2]
    kinds = 2 * (L_CUTS + F_CUTS)
    held = pl.pallas_call(
        fused_kernel,
        out_shape=(
            pltpu.VMEM(rhs_top.shape, jnp.float32),
            pltpu.VMEM(rhs_rest.shape, jnp.float32),
            pltpu.VMEM((parts, panel, trail), factor_t.dtype),
            pltpu.VMEM((4 * panel, width), jnp.bfloat16),
        ),
        in_specs=[pl.BlockSpec(memory_space=pl.ANY)] * 4,
        out_specs=[pl.BlockSpec(memory_space=pltpu.VMEM)] * 4,
        scratch_shapes=[
            pltpu.VMEM((parts, panel, panel), linv_t.dtype),
            pltpu.SemaphoreType.DMA((kinds, devices)),
            pltpu.SemaphoreType.DMA((5, kinds, devices // 2)),
            pltpu.SemaphoreType.DMA((TOP_CUTS + 3,)),
        ],
        compiler_params=pltpu.CompilerParams(
            collective_id=0, has_side_effects=True, vmem_limit_bytes=30 << 20
        ),
    )(linv_t, rhs_top, factor_t, rhs_rest)
    return pl.pallas_call(
        store_kernel,
        out_shape=(
            jax.ShapeDtypeStruct(rhs_top.shape, jnp.float32),
            jax.ShapeDtypeStruct(rhs_rest.shape, jnp.float32),
        ),
        in_specs=[pl.BlockSpec(memory_space=pltpu.VMEM)] * 4,
        out_specs=[pl.BlockSpec(memory_space=pl.ANY)] * 2,
        scratch_shapes=[
            pltpu.VMEM(rhs_rest.shape, jnp.float32),
            pltpu.SemaphoreType.DMA((1 + STORE_CUTS,)),
        ],
        compiler_params=pltpu.CompilerParams(vmem_limit_bytes=30 << 20),
    )(*(pltpu.with_memory_space_constraint(array, pltpu.VMEM) for array in held))


def solution(mesh):
    devices = mesh.shape["ang"]
    if mesh.shape["row"] == 1 and devices == 8 * LEVELS:
        body = functools.partial(fused_body, devices)
    else:
        body = general_body
    return jax.shard_map(
        body,
        mesh=mesh,
        in_specs=(
            P(None, "ang", "row"),
            P(None, "row", "ang"),
            P(None, "ang", "row"),
            P(None, "row", "ang"),
        ),
        out_specs=(P(None, "row", "ang"), P(None, "row", "ang")),
        check_vma=False,
    )
```
